128 devices in a mesh: grp: 8 (over z, core), mem: 16 (over y, x).
Axes of the slice: x: 4, y: 4, z: 4, core: 2. Of those that a mesh axis runs over, the one named last changes fastest.
Arguments:
- embeddings: bfloat16 [49152, 1024], P(('grp', 'mem')), may hold values from -6 to 6
- row_target: int32 [49152, 1], P(('grp', 'mem')), may hold values from 0 to 127; in each aligned block of 384 rows (0 to 383, 384 to 767, ...) at most 6 rows name the same one
Outputs:
- best_cosine: float32 [49152], P(('grp', 'mem'))
The draws below stay inside these ranges and needn't reach their ends.
Inputs may be any that keep to these rules, and one draw needn't show every extreme that they name: `row_target`: among the rows of one device no owner device is named by more than 6 rows, a bound that some block reaches.
All inputs are finite; a program needn't handle non-finite values.
Results may differ from the reference program's by a relative error of at most 0.0012.
Values may be sent and summed in bfloat16 or wider, within the bound.
No kernel may reach another device: no remote copies, remote signals or barrier semaphores. Data moves between devices by JAX's collectives and lax.ppermute only.
A program may use at most 128 MiB of HBM per device.

```python
import math
import jax
import jax.numpy as jnp
import numpy as np
from jax import lax

D = 1024
ROW_DEV = 384
CAP = 6
SLOTS = 768
ROWS = 49152
N_GRP = 8
N_MEM = 16
DEVICES = 128


def block_scale(rng, extent, pieces, smallest, top_value):
    factor_of = 1.0
    for dim, shards_of in pieces:
        heights = jax.random.uniform(jax.random.fold_in(jax.random.fold_in(rng, 6), dim), (shards_of,), jnp.float32, smallest / len(pieces), top_value / len(pieces))
        factor_of = factor_of * jnp.repeat(jnp.exp(heights), extent[dim] // shards_of).reshape((-1,) + (1,) * (len(extent) - 1 - dim))
    return factor_of


def deal_out(stream_key, own, number, rows, amount, top, bound, lean):
    order = jax.random.permutation(stream_key, amount)
    packed, usual = load_shares(amount, rows * top, bound, lean, True), load_shares(amount, rows * top, bound, lean, False)
    places = jnp.arange(amount)

    def named(tallies, offset_by):
        used = int((tallies > 0).sum())
        fixed = max(1, used // 4)
        moved = fixed + (places - fixed + offset_by * (used - fixed)) % max(1, amount - fixed)
        return jnp.zeros((amount,), jnp.int32).at[order[jnp.where(places < fixed, places, moved)]].set(jnp.asarray(tallies, jnp.int32))

    tallies = jnp.where(number % 4 == 0, named(packed, number // 4), named(usual, number - number // 4 - 1))
    mixed = jax.random.permutation(jax.random.fold_in(own, 3), amount)
    giver, receiver = mixed[0:amount // 2 * 2:2], mixed[1:amount // 2 * 2:2]
    room = jnp.minimum(tallies[giver] - 1, bound - tallies[receiver]) // 2
    room = jnp.where((giver == order[0]) | (receiver == order[0]) | (tallies[receiver] == 0), 0, jnp.maximum(room, 0))
    moved = jax.random.randint(jax.random.fold_in(own, 4), (amount // 2,), 0, 1 << 20) % (room + 1)
    tallies = tallies.at[giver].add(-moved).at[receiver].add(moved)
    labels = jnp.searchsorted(jnp.cumsum(tallies), jnp.arange(rows * top), side="right").astype(jnp.int32)
    table = labels.reshape(top, rows).T
    table = table[jax.random.permutation(jax.random.fold_in(own, 1), rows)]
    offset_by = jax.random.randint(jax.random.fold_in(own, 2), (rows, 1), 0, top)
    return jnp.take_along_axis(table, (jnp.arange(top)[None, :] + offset_by) % top, axis=1)


def load_shares(number_of, total, bound, skew, full):
    portions = [(1 << 20) // math.isqrt(grade ** skew) + 1 for grade in range(1, number_of + 1)]
    largest = bound if full else min(bound, max(-(-total // number_of), total * portions[0] // sum(portions)))
    least = 1 if total - largest >= number_of - 1 else 0
    holding, rest = [largest] + [least] * (number_of - 1), total - largest - least * (number_of - 1)
    while rest > 0:
        movable = [i for i in range(1, number_of) if holding[i] < largest] or [i for i in range(1, number_of) if holding[i] < bound]
        whole, left = sum([portions[i] for i in movable]), rest
        for i in movable:
            addition = min(bound - holding[i], max(1, left * portions[i] // whole), rest)
            holding[i] = holding[i] + addition
            rest = rest - addition
    return np.array(holding)


def normal_values(stream_key, dims, scale, limit, split=(), kind=jnp.bfloat16):
    values = jax.random.normal(stream_key, dims, jnp.float32) * scale
    if len(split) > 0:
        values = block_scale(stream_key, dims, split, -0.22, 0.18) * values
    return jnp.clip(values, min=-limit, max=limit).astype(kind)


def setup_inputs(seed: int = 0) -> dict:
    keys = jax.random.split(jax.random.key(seed), 3)
    embeddings = normal_values(keys[0], (ROWS, D), 1.0, 6.0, ((0, 128),))
    row_target_keys = jax.random.split(jax.random.fold_in(keys[1], 1), ROWS // ROW_DEV)
    row_target_turns = jax.random.permutation(jax.random.fold_in(keys[1], 3), ROWS // ROW_DEV)
    row_target = jax.vmap(lambda own, number: deal_out(jax.random.fold_in(keys[1], 2), own, number, ROW_DEV, DEVICES, 1, CAP, 2))(row_target_keys, row_target_turns).reshape((ROWS, 1))
    return dict(embeddings=embeddings, row_target=row_target)


def reference(embeddings, row_target):
    values = embeddings.astype(jnp.float32)
    inv_norm = lax.rsqrt(lax.optimization_barrier(jnp.mean(values * values, axis=1, keepdims=True)) + 1e-06) * (1.0 / math.sqrt(D))
    unit_rows = (values * inv_norm).astype(jnp.bfloat16)
    target = row_target[:, 0].reshape(DEVICES, ROW_DEV)
    onehot = (target[:, :, None] == jnp.arange(DEVICES, dtype=jnp.int32)[None, None, :]).astype(jnp.int32)
    running = jnp.cumsum(onehot, axis=1)
    slot_index = lax.optimization_barrier(jnp.sum(onehot * running, axis=2)) - 1
    source = jnp.arange(DEVICES, dtype=jnp.int32)[:, None]
    position = (source * CAP + slot_index).reshape(-1).astype(jnp.int32)
    owner_dev = target.reshape(-1).astype(jnp.int32)
    held_rows = jnp.zeros((DEVICES, SLOTS, D), jnp.bfloat16).at[owner_dev, position].set(unit_rows)
    held_ident = jnp.full((DEVICES, SLOTS), ROWS, jnp.int32).at[owner_dev, position].set(jnp.arange(ROWS, dtype=jnp.int32))
    grouped = held_rows.reshape(N_GRP, N_MEM * SLOTS, D)
    grouped_ident = held_ident.reshape(N_GRP, N_MEM * SLOTS)

    def per_device(device):
        own_block = held_rows[device]
        row_ident = held_ident[device]
        group_index = device // N_MEM
        others = grouped[group_index]
        other_ident = grouped_ident[group_index]
        cosines = lax.dot_general(own_block, others, (((1,), (1,)), ((), ())), preferred_element_type=jnp.float32)
        keep_mask = (other_ident[None, :] < ROWS) & (other_ident[None, :] != row_ident[:, None])
        return jnp.maximum(lax.optimization_barrier(jnp.max(jnp.where(keep_mask, cosines, -1.0), axis=1)), -1.0)
    best_value = lax.map(per_device, jnp.arange(DEVICES, dtype=jnp.int32))
    return jnp.zeros((ROWS,), jnp.float32).at[held_ident.reshape(-1)].set(best_value.reshape(-1), mode='drop')
```

```python
import math

import jax
import jax.numpy as jnp
import numpy as np
from jax import lax
from jax.experimental import pallas as pl
from jax.experimental.pallas import tpu as pltpu
from jax.sharding import PartitionSpec as P

AXES = ("grp", "mem")
ROWS = 384
WIDTH = 1024
PAD = 16
PART = 128
NONE = -4.0

SHIFT = {
    "O": (0, 0, 0), "X": (0, 0, 1), "Y": (0, 1, 0), "Z": (1, 0, 0), "D": (3, 3, 3),
    "XX": (0, 0, 2), "YY": (0, 2, 0), "ZZ": (2, 0, 0),
    "DX": (3, 3, 2), "DY": (3, 2, 3), "DZ": (2, 3, 3),
}
BOTH = ("O", "X", "Y", "Z", "XX", "YY", "ZZ")
FIRST = ["O", "X", "Y", "Z"]
JOBS_A = [("X", "O"), ("Y", "O"), ("Z", "O"), ("D", "O"), ("D", "X"), ("D", "Y"), ("D", "Z"),
          ("Y", "X"), ("Z", "X"), ("Z", "Y")]
JOBS_B = [("XX", "O"), ("YY", "O"), ("ZZ", "O"), ("YY", "X"), ("ZZ", "X"), ("DX", "X"),
          ("XX", "Y"), ("ZZ", "Y"), ("DX", "Y"), ("DY", "Y"), ("XX", "Z"), ("YY", "Z"),
          ("DX", "Z"), ("DY", "Z"), ("DZ", "Z")]
JOBS_C = [("YY", "XX"), ("ZZ", "XX"), ("ZZ", "YY"), ("DX", "XX"), ("DY", "YY"), ("DZ", "ZZ"),
          ("DY", "XX"), ("DZ", "YY"), ("DX", "ZZ")]
PARTS = [((1, 1, 0), "DX"), ((1, 0, 1), "DY"), ((0, 1, 1), "DZ")]


def dev(z, y, x, c):
    return ((z % 4) * 2 + c % 2) * 16 + (y % 4) * 4 + x % 4


POS = [(z, c, y, x) for z in range(4) for c in range(2) for y in range(4) for x in range(4)]


def shift_perm(s):
    return [(dev(z + s[0], y + s[1], x + s[2], c), dev(z, y, x, c)) for z, c, y, x in POS]


SWAP = [(dev(z, y, x, 1 - c), dev(z, y, x, c)) for z, c, y, x in POS]


def part_core(z, c):
    return c if z % 4 < 2 else 1 - c


def part_perm(via, s):
    return [(dev(z + via[0], y + via[1], x + via[2], part_core(z + s[0], c)), dev(z, y, x, c))
            for z, c, y, x in POS]


def prep_kernel(emb_ref, tgt_ref, out_ref):
    values = emb_ref[...].astype(jnp.float32)
    mean = jnp.sum(values * values, axis=1, keepdims=True) * (1.0 / WIDTH)
    inv = lax.rsqrt(mean + 1e-06) * (1.0 / math.sqrt(WIDTH))
    out_ref[0:ROWS, :] = (values * inv).astype(jnp.bfloat16)
    ids = (tgt_ref[...] >> 4).astype(jnp.float32)
    out_ref[ROWS:ROWS + PAD, :] = jnp.zeros((PAD, WIDTH), jnp.bfloat16)
    out_ref[ROWS:ROWS + PAD, 0:ROWS] = jnp.broadcast_to(ids, (PAD, ROWS)).astype(jnp.bfloat16)


def prep(embeddings, target_row):
    return pl.pallas_call(
        prep_kernel,
        out_shape=jax.ShapeDtypeStruct((ROWS + PAD, WIDTH), jnp.bfloat16),
        name="prep",
    )(embeddings, target_row)


def slot_table(names):
    slots = {}
    for n in names:
        if n in BOTH:
            slots[n] = len(slots)
            slots[n + "'"] = len(slots)
    for n in names:
        if n not in BOTH:
            slots[n] = len(slots)
    return slots


def make_phase(slots, jobs, left, self_job, parts, final):
    n = len(slots)
    lefts = {s: i for i, s in enumerate(left)}
    n_left = len(left)
    np_ = len(parts)

    def kernel(*refs):
        jobs_ref, refs = refs[0], refs[1:]
        if final:
            dst_ref, refs = refs[0], refs[1:]
        blocks, refs = refs[:n], refs[n:]
        part_refs, refs = refs[:np_], refs[np_:]
        if final:
            prev, refs = refs[0], refs[1:]
        out_ref, refs = refs[0], refs[1:]
        rows, ids, id_col, acc_r, acc_c, part_rows, sem = refs

        copies = []
        for i in range(n):
            copies.append(pltpu.make_async_copy(
                blocks[i].at[pl.ds(0, ROWS), :], rows.at[pl.ds(i * ROWS, ROWS), :], sem.at[2 * i]))
            copies.append(pltpu.make_async_copy(
                blocks[i].at[pl.ds(ROWS, PAD), pl.ds(0, ROWS)], ids.at[i], sem.at[2 * i + 1]))
        for i in range(np_):
            copies.append(pltpu.make_async_copy(part_refs[i], part_rows.at[i], sem.at[2 * n + i]))
        for c in copies:
            c.start()
        acc_r[...] = jnp.full(acc_r.shape, NONE, jnp.float32)
        acc_c[...] = jnp.full(acc_c.shape, NONE, jnp.float32)
        for c in copies:
            c.wait()

        def id_row(slot):
            return ids[slot].astype(jnp.float32)[0:1, :]

        for name, i in lefts.items():
            row = id_row(slots[name])
            for k in range(3):
                tile = jnp.broadcast_to(row[:, 128 * k:128 * k + 128], (128, 128))
                id_col[i, 128 * k:128 * k + 128, :] = tile.T

        def product(lhs, rhs):
            return lax.dot_general(lhs, rhs, (((1,), (1,)), ((), ())),
                                   preferred_element_type=jnp.float32)

        def job(a, al, b, diagonal):
            lhs = rows[pl.ds(pl.multiple_of(a * ROWS, ROWS), ROWS), :]
            rhs = rows[pl.ds(pl.multiple_of(b * ROWS, ROWS), 2 * ROWS), :]
            cos = product(lhs, rhs)
            own = id_col[al]
            best = acc_r[al]
            for h in range(2):
                other = ids[b + h].astype(jnp.float32)[0:1, :]
                for k in range(3):
                    lo = h * ROWS + 128 * k
                    keep = own == other[:, 128 * k:128 * k + 128]
                    if diagonal and h == 0:
                        i0 = lax.broadcasted_iota(jnp.int32, (ROWS, 128), 0)
                        i1 = lax.broadcasted_iota(jnp.int32, (ROWS, 128), 1) + 128 * k
                        keep = keep & (i0 != i1)
                    val = jnp.where(keep, cos[:, lo:lo + 128], NONE)
                    best = jnp.maximum(best, val)
                    top = jnp.max(val.reshape(ROWS // 8, 8, 128), axis=0)
                    acc_c[b + h, :, 128 * k:128 * k + 128] = jnp.maximum(
                        acc_c[b + h, :, 128 * k:128 * k + 128], top)
            acc_r[al] = best

        if self_job:
            job(slots["O"], lefts["O"], slots["O"], True)

        def step(j, carry):
            job(jobs_ref[3 * j], jobs_ref[3 * j + 1], jobs_ref[3 * j + 2], False)
            return carry

        lax.fori_loop(0, len(jobs), step, 0)

        part_top = []
        for i, (_, partner) in enumerate(parts):
            s = slots[partner]
            lhs = part_rows[i, 0:PART, :]
            row = part_rows[i, PART:PART + PAD, 0:PART].astype(jnp.float32)[0:1, :]
            own = jnp.broadcast_to(row, (PART, PART)).T
            cos = product(lhs, rows[s * ROWS:s * ROWS + ROWS, :])
            other = id_row(s)
            best = jnp.full((PART, 128), NONE, jnp.float32)
            for k in range(3):
                keep = own == other[:, 128 * k:128 * k + 128]
                val = jnp.where(keep, cos[:, 128 * k:128 * k + 128], NONE)
                best = jnp.maximum(best, val)
                top = jnp.max(val.reshape(PART // 8, 8, 128), axis=0)
                acc_c[s, :, 128 * k:128 * k + 128] = jnp.maximum(
                    acc_c[s, :, 128 * k:128 * k + 128], top)
            part_top.append(jnp.max(best.T, axis=0, keepdims=True))

        if final:
            out_ref[...] = jnp.full(out_ref.shape, NONE, jnp.float32)
        for name, s in slots.items():
            top = jnp.max(acc_c[s], axis=0, keepdims=True)
            if name in lefts:
                cols = [jnp.max(acc_r[lefts[name], 128 * k:128 * k + 128, :].T, axis=0, keepdims=True)
                        for k in range(3)]
                top = jnp.maximum(top, jnp.concatenate(cols, axis=1))
            if final:
                if s < prev.shape[0]:
                    top = jnp.maximum(top, prev[s])
                out_ref[dst_ref[s]] = top
            else:
                out_ref[s] = top
        if final:
            for i in range(np_):
                out_ref[dst_ref[n + i], :, PART * i:PART * i + PART] = part_top[i]

    out_rows = 128 if final else n
    table = np.array([[slots[a], lefts[a], slots[b]] for a, b in jobs], np.int32).reshape(-1)
    scratch = [
        pltpu.VMEM((n * ROWS, WIDTH), jnp.bfloat16),
        pltpu.VMEM((n, PAD, ROWS), jnp.bfloat16),
        pltpu.VMEM((n_left, ROWS, 128), jnp.float32),
        pltpu.VMEM((n_left, ROWS, 128), jnp.float32),
        pltpu.VMEM((n, 8, ROWS), jnp.float32),
        pltpu.VMEM((max(np_, 1), PART + PAD, WIDTH), jnp.bfloat16),
        pltpu.SemaphoreType.DMA((2 * n + max(np_, 1),)),
    ]

    def call(blocks, part_blocks=(), dst=None, prev=None):
        smem = pl.BlockSpec(memory_space=pltpu.MemorySpace.SMEM)
        specs, args = [smem], [jnp.asarray(table)]
        if final:
            specs.append(smem)
            args.append(dst)
        specs += [pl.BlockSpec(memory_space=pl.ANY)] * (n + np_)
        args += list(blocks) + list(part_blocks)
        if final:
            specs.append(pl.BlockSpec(memory_space=pltpu.MemorySpace.VMEM))
            args.append(prev)
        pairs = len(jobs) * 2 + (2 if self_job else 0)
        return pl.pallas_call(
            kernel,
            in_specs=specs,
            out_specs=pl.BlockSpec(memory_space=pltpu.MemorySpace.VMEM),
            out_shape=jax.ShapeDtypeStruct((out_rows, 1, ROWS), jnp.float32),
            scratch_shapes=scratch,
            cost_estimate=pl.CostEstimate(
                flops=2 * pairs * ROWS * ROWS * WIDTH, transcendentals=0,
                bytes_accessed=n * ROWS * WIDTH * 2),
            name="pairs_last" if final else "pairs_first",
        )(*args)

    return call


SLOTS_A = slot_table(["O", "X", "Y", "Z", "D"])
NAMES_B = ["O", "X", "Y", "Z", "XX", "YY", "ZZ", "D", "DX", "DY", "DZ"]
SLOTS_B = slot_table(NAMES_B)


def target_table():
    table = np.zeros((128, len(SLOTS_B) + len(PARTS)), np.int32)
    for z, c, y, x in POS:
        d = dev(z, y, x, c)
        for name, s in SLOTS_B.items():
            dz, dy, dx = SHIFT[name.rstrip("'")]
            table[d, s] = dev(z + dz, y + dy, x + dx, 1 - c if name.endswith("'") else c)
        for i, ((dz, dy, dx), _) in enumerate(PARTS):
            table[d, len(SLOTS_B) + i] = dev(z + dz, y + dy, x + dx, part_core(z + dz, c))
    return table


TARGETS = target_table()


def per_device(embeddings, row_target):
    own = prep(embeddings, row_target.reshape(1, ROWS))
    held = {"O": own}

    def move(value, perm):
        return lax.ppermute(value, AXES, perm)

    for n in ("X", "Y", "Z", "D"):
        held[n] = move(own, shift_perm(SHIFT[n]))
    held["O'"] = move(own, SWAP)
    for n, src, via in (("DX", "D", (0, 0, 3)), ("DY", "D", (0, 3, 0)), ("DZ", "D", (3, 0, 0)),
                        ("XX", "X", (0, 0, 1)), ("YY", "Y", (0, 1, 0)), ("ZZ", "Z", (1, 0, 0))):
        held[n] = move(held[src], shift_perm(via))
    for n in ("X", "Y", "Z", "XX", "YY", "ZZ"):
        held[n + "'"] = move(held[n], SWAP)

    def part(name, i):
        block = held[name]
        id_rows = jnp.pad(block[ROWS:, PART * i:PART * i + PART], ((0, 0), (0, WIDTH - PART)))
        return jnp.concatenate([block[PART * i:PART * i + PART], id_rows], axis=0)

    parts = [move(part("Y", 0), part_perm((1, 0, 0), PARTS[0][0])),
             move(part("Z", 1), part_perm((0, 0, 1), PARTS[1][0])),
             move(part("X", 2), part_perm((0, 1, 0), PARTS[2][0]))]

    first = make_phase(SLOTS_A, JOBS_A, ["O", "X", "Y", "Z", "D"], True, [], False)
    prev = first([held[s] for s in SLOTS_A])
    lead = [SLOTS_A[s] for s in SLOTS_A if s != "D"]
    me = lax.axis_index("grp") * 16 + lax.axis_index("mem")
    dst = lax.dynamic_slice(jnp.asarray(TARGETS), (me, 0), (1, TARGETS.shape[1]))[0]
    prev_rows = jnp.concatenate(
        [prev[:len(lead)], jnp.full((6, 1, ROWS), NONE, jnp.float32), prev[SLOTS_A["D"]:]], axis=0)
    last = make_phase(SLOTS_B, JOBS_B + JOBS_C, NAMES_B, False, PARTS, True)
    sent = last([held[s] for s in SLOTS_B], parts, dst, prev_rows)
    back = lax.all_to_all(sent, AXES, split_axis=0, concat_axis=0, tiled=True)
    return jnp.maximum(jnp.max(back[:, 0, :], axis=0), -1.0)


def solution(mesh):
    in_specs = (P(AXES, None), P(AXES, None))
    return jax.shard_map(
        per_device, mesh=mesh, in_specs=in_specs, out_specs=P(AXES), check_vma=False
    )
```
